32 devices in a mesh: dp: 8 (over z, x), seq: 4 (over y, core).
Axes of the slice: x: 2, y: 2, z: 4, core: 2. Of those that a mesh axis runs over, the one named last changes fastest.
Arguments:
- enc_rows: bfloat16 [32, 256, 1280], P('dp', 'seq'), may hold values from -100 to 100
- out_weight: bfloat16 [1280, 512], replicated, may hold values from -3 to 3
- labels: int32 [32, 63], P('dp'), may hold values from 1 to 511
- label_count: int32 [32], P('dp'), may hold values from 1 to 63, as said below
- frame_count: int32 [32], P('dp'), may hold values from 128 to 256, as said below
Outputs:
- logit_grad: bfloat16 [32, 256, 512], P('dp', 'seq')
- row_grad: bfloat16 [32, 256, 1280], P('dp', 'seq')
- weight_grad: float32 [1280, 512], P('dp', 'seq')
The draws below stay inside these ranges and needn't reach their ends.
Inputs may be any that keep to these rules, and one draw needn't show every extreme that they name: `labels`: character ids; id 0 is the blank and never appears. `label_count`: some utterance has 63 labels in every draw. `frame_count`: some utterance has 256 frames in every draw.
All inputs are finite; a program needn't handle non-finite values.
Results may differ from the reference program's by a relative error of at most 0.0043.
Values sent between devices are 32-bit elements; how exact they have to be, the bound alone decides.
A program may use at most 64 MiB of HBM per device.

```python
import math
import jax
import jax.numpy as jnp
from jax import lax

D = 1280
V = 512
SEQS = 4
FRAMES = 256
L = 63
BATCH = 32
N_DP = 8


def weight_table(key):
    spread = 3.0 / math.sqrt(D)
    drawn = jax.random.normal(jax.random.fold_in(key, 11), (D, V), jnp.float32) * spread
    return jnp.clip(drawn, -3.0, 3.0)


def draw_out_weight(key, part):
    return weight_table(key).astype(jnp.bfloat16)


def draw_enc_rows(key, part):
    base_rows = jnp.clip(jax.random.normal(jax.random.fold_in(key, 21), (BATCH, FRAMES, D), jnp.float32), -6.0, 6.0)
    return jnp.clip(base_rows, -100.0, 100.0).astype(jnp.bfloat16)


def forced_most(key, lowest, highest):
    drawn = jax.random.randint(jax.random.fold_in(key, 31), (BATCH,), lowest, highest + 1)
    forced_spot = jax.random.randint(jax.random.fold_in(key, 32), (), 0, BATCH)
    return jnp.where(jnp.arange(BATCH) == forced_spot, highest, drawn).astype(jnp.int32)


def draw_frame_count(key, part):
    return forced_most(jax.random.fold_in(key, 51), FRAMES // 2, FRAMES)


def draw_label_count(key, part):
    return forced_most(jax.random.fold_in(key, 41), 1, L)


def place_ends(values, own_key, smallest, top_value):
    longest = values.shape.index(max(values.shape))
    spots = []
    for shift in (0, 1):
        where = [jax.random.randint(jax.random.fold_in(own_key, axis), (), 0, length) for axis, length in enumerate(values.shape)]
        where[longest] = (where[longest] + shift) % values.shape[longest]
        spots.append(tuple(where))
    return values.at[spots[0]].set(smallest).at[spots[1]].set(top_value)


def setup_inputs(seed: int = 0) -> dict:
    streams_of = jax.random.split(jax.random.key(seed), 6)
    return {
        "enc_rows": draw_enc_rows(jax.random.fold_in(streams_of[5], 71), 0),
        "out_weight": draw_out_weight(jax.random.fold_in(streams_of[5], 71), 0),
        "labels": place_ends(jax.random.randint(streams_of[2], (BATCH, L), 1, V), jax.random.fold_in(streams_of[2], 1), 1, V - 1).astype(jnp.int32),
        "label_count": draw_label_count(jax.random.fold_in(streams_of[5], 71), 0),
        "frame_count": draw_frame_count(jax.random.fold_in(streams_of[5], 71), 0),
    }


negative_fill = -1.0e30


def merge_three(first_term, second_term, third_term):
    highest = jnp.maximum(jnp.maximum(first_term, second_term), third_term)
    return highest + jnp.log(jnp.exp(first_term - highest) + jnp.exp(second_term - highest) + jnp.exp(third_term - highest))


def shift_right(values, amount):
    filler = jnp.full((values.shape[0], amount), negative_fill, jnp.float32)
    return jnp.concatenate([filler, values[:, :-amount]], axis=1)


def shift_left(values, amount):
    filler = jnp.full((values.shape[0], amount), negative_fill, jnp.float32)
    return jnp.concatenate([values[:, amount:], filler], axis=1)


def advance(current, emission, usable, allowed):
    from_one = shift_right(current, 1)
    from_two = jnp.where(allowed, shift_right(current, 2), negative_fill)
    fresh = merge_three(current, from_one, from_two) + emission
    return jnp.where(usable[:, None], fresh, current)


def retreat(current, emission, usable, allowed_next):
    summed = current + emission
    next_one = shift_left(summed, 1)
    next_two = jnp.where(allowed_next, shift_left(summed, 2), negative_fill)
    fresh = merge_three(summed, next_one, next_two)
    return jnp.where(usable[:, None], fresh, current)


def lattice(labels, label_count):
    utterances, length = labels.shape
    states_wide = 2 * length + 2
    blanks = jnp.zeros((utterances, length + 1), jnp.int32)
    chars = jnp.concatenate([labels, jnp.full((utterances, 1), -1, jnp.int32)], axis=1)
    extended = jnp.stack([blanks, chars], axis=2).reshape(utterances, states_wide)
    earlier = jnp.concatenate([jnp.full((utterances, 2), -2, jnp.int32), extended[:, :-2]], axis=1)
    positions = jnp.arange(states_wide, dtype=jnp.int32)[None, :]
    allowed = (positions % 2 == 1) & (positions >= 3) & (extended != earlier)
    allowed_next = jnp.concatenate([allowed[:, 2:], jnp.zeros((utterances, 2), jnp.bool_)], axis=1)
    zeros_row = jnp.zeros((utterances, states_wide), jnp.float32)
    initial = jnp.where(positions == 0, zeros_row, negative_fill)
    doubled = 2 * label_count[:, None]
    closing = jnp.where((positions == doubled) | (positions == doubled - 1), zeros_row, negative_fill)
    return allowed, allowed_next, initial, closing


def emissions(logprob, labels):
    utterances, frames, vocabulary = logprob.shape
    length = labels.shape[1]
    char_index = jnp.concatenate([jnp.zeros((utterances, 1), jnp.int32), labels], axis=1)
    picked = jnp.take_along_axis(logprob, jnp.broadcast_to(char_index[:, None, :], (utterances, frames, length + 1)), axis=2)
    blank_part = jnp.broadcast_to(picked[:, :, :1], picked.shape)
    label_part = jnp.concatenate([picked[:, :, 1:], jnp.full((utterances, frames, 1), negative_fill, jnp.float32)], axis=2)
    emission = jnp.stack([blank_part, label_part], axis=3).reshape(utterances, frames, 2 * length + 2)
    return jnp.swapaxes(emission, 0, 1), char_index


def forward_pass(initial, emission, usable, allowed):
    def frame_step(current, inputs):
        fresh = advance(current, inputs[0], inputs[1], allowed)
        return fresh, fresh
    return lax.scan(frame_step, initial, (emission, usable))


def backward_pass(closing, emission, usable, allowed_next):
    def frame_step(current, inputs):
        return retreat(current, inputs[0], inputs[1], allowed_next), current
    return lax.scan(frame_step, closing, (emission, usable), reverse=True)


def gradients(logprob, forward_states, backward_states, usable, char_index):
    frames, utterances, states_wide = forward_states.shape
    summed = forward_states + backward_states
    highest = jnp.max(summed, axis=2, keepdims=True)
    log_total = highest + jnp.log(jnp.sum(jnp.exp(summed - highest), axis=2, keepdims=True))
    posterior = jnp.exp(summed - log_total) * usable[:, :, None].astype(jnp.float32)
    paired = posterior.reshape(frames, utterances, states_wide // 2, 2)
    blank_mass = jnp.sum(paired[:, :, :, 0], axis=2, keepdims=True)
    occupancy = jnp.concatenate([blank_mass, paired[:, :, :-1, 1]], axis=2)
    vocabulary = logprob.shape[2]
    one_hot = (char_index[:, :, None] == jnp.arange(vocabulary, dtype=jnp.int32)[None, None, :]).astype(jnp.float32)
    char_mass = jnp.einsum("fup,upv->ufv", occupancy, one_hot, precision=lax.Precision.HIGHEST)
    keep = jnp.swapaxes(usable, 0, 1)[:, :, None].astype(jnp.float32)
    return ((jnp.exp(logprob) - char_mass) * keep).astype(jnp.bfloat16)


def reference(enc_rows, out_weight, labels, label_count, frame_count):
    def one_block(inputs):
        block_rows, block_labels, block_lcount, block_fcount = inputs
        utterances, frames, width_rows = block_rows.shape
        flat_rows = block_rows.reshape(utterances * frames, width_rows)
        logits = jnp.dot(flat_rows, out_weight, preferred_element_type=jnp.float32).reshape(utterances, frames, -1)
        logprob = jax.nn.log_softmax(logits, axis=-1)
        emission, char_index = emissions(logprob, block_labels)
        allowed, allowed_next, initial, closing = lattice(block_labels, block_lcount)
        usable = jnp.arange(frames, dtype=jnp.int32)[:, None] < block_fcount[None, :]
        forward_states = forward_pass(initial, emission, usable, allowed)[1]
        backward_states = backward_pass(closing, emission, usable, allowed_next)[1]
        logit_grad = gradients(logprob, forward_states, backward_states, usable, char_index)
        flat_grad = logit_grad.reshape(utterances * frames, -1)
        row_grad = lax.dot_general(flat_grad, out_weight, (((1,), (1,)), ((), ())), preferred_element_type=jnp.float32)
        row_grad = row_grad.astype(jnp.bfloat16).reshape(utterances, frames, width_rows)
        weight_term = lax.dot_general(flat_rows, flat_grad, (((0,), (0,)), ((), ())), preferred_element_type=jnp.float32)
        return logit_grad, row_grad, weight_term

    blocks = (enc_rows.reshape(N_DP, SEQS, FRAMES, D), labels.reshape(N_DP, SEQS, L),
              label_count.reshape(N_DP, SEQS), frame_count.reshape(N_DP, SEQS))
    logit_grad, row_grad, weight_terms = lax.map(one_block, blocks)
    weight_grad = jnp.sum(weight_terms, axis=0) / BATCH
    return logit_grad.reshape(BATCH, FRAMES, V), row_grad.reshape(BATCH, FRAMES, D), weight_grad
```

```python
import functools

import jax
import jax.numpy as jnp
from jax import lax
from jax.experimental import pallas as pl
from jax.experimental.pallas import tpu as pltpu
from jax.sharding import PartitionSpec as P

negative_fill = -1e30
LANES = 128
SPLIT = 2
UNROLL = 16
MESH = pl.DeviceIdType.MESH
BOTH_LAST = (((1,), (1,)), ((), ()))


def three_parts(values):
    high = values.astype(jnp.bfloat16)
    rest = values - high.astype(jnp.float32)
    middle = rest.astype(jnp.bfloat16)
    low = (rest - middle.astype(jnp.float32)).astype(jnp.bfloat16)
    return high, middle, low


def emission_kernel(seq_count, utterances, enc_ref, weight_ref, chars_ref,
                    logprob_ref, gathered_ref, send_sems, recv_sems):
    me = lax.axis_index("seq")
    barrier = pltpu.get_barrier_semaphore()
    for step in range(1, seq_count):
        peer = lax.rem(me + step, seq_count)
        pl.semaphore_signal(barrier, inc=1, device_id={"seq": peer}, device_id_type=MESH)
    frames = enc_ref.shape[0] // utterances
    vocabulary = weight_ref.shape[1]
    groups = gathered_ref.shape[1]
    pack = utterances // groups
    logits = jnp.dot(enc_ref[...], weight_ref[...], preferred_element_type=jnp.float32)
    highest = jnp.max(logits, axis=1, keepdims=True)
    total = jnp.sum(jnp.exp(logits - highest), axis=1, keepdims=True)
    logprob = logits - (highest + jnp.log(total))
    rows = lax.broadcasted_iota(jnp.int32, (vocabulary, LANES), 0)
    for group in range(groups):
        picked = jnp.zeros((frames, LANES), jnp.float32)
        for inner in range(pack):
            utterance = group * pack + inner
            one_hot = jnp.where(
                rows == chars_ref[pl.ds(utterance, 1), :], 1.0, 0.0
            ).astype(jnp.bfloat16)
            mine = logprob[utterance * frames:(utterance + 1) * frames]
            for part in three_parts(mine):
                picked += jnp.dot(part, one_hot, preferred_element_type=jnp.float32)
        gathered_ref[me, group] = picked
    logprob_ref[...] = logprob
    pl.semaphore_wait(barrier, seq_count - 1)
    copies = []
    for step in range(1, seq_count):
        peer = lax.rem(me + step, seq_count)
        copy = pltpu.make_async_remote_copy(
            src_ref=gathered_ref.at[me],
            dst_ref=gathered_ref.at[me],
            send_sem=send_sems.at[step - 1],
            recv_sem=recv_sems.at[step - 1],
            device_id={"seq": peer},
            device_id_type=MESH,
        )
        copy.start()
        copies.append(copy)
    for copy in copies:
        copy.wait()


def take_lanes(values, index):
    return jnp.take_along_axis(values, index, axis=1)


def lattice_kernel(length, utterances, place_ref, gathered_ref, meta_ref, logprob_ref, enc_ref,
                   weight_ref, logit_ref, row_ref, term_ref, level_ref, factor_ref, mass_ref):
    seq_count, groups, frames = gathered_ref.shape[:3]
    steps = seq_count * frames
    rows = 2 * utterances
    slots = length + 1
    pack = utterances // groups
    span = LANES * SPLIT
    shape = (rows, LANES)
    row = lax.broadcasted_iota(jnp.int32, shape, 0)
    lane = lax.broadcasted_iota(jnp.int32, shape, 1)
    forward = row < utterances
    utterance = lax.rem(row, utterances)
    offset = lax.rem(utterance, pack) * slots
    label_rows = meta_ref[0]
    label_count = meta_ref[1]
    frame_count = meta_ref[2]
    first_usable = jnp.where(forward, 0, steps - frame_count)

    label_index, label_fill, jump_fill, label_start = [], [], [], []
    blank_fill, blank_start, label_chars = [], [], []
    for r in range(SPLIT):
        place = lane * SPLIT + r
        j = jnp.where(forward, place, span - 1 - place)
        real = j < length
        label_index.append(offset + jnp.clip(j, 0, slots - 1))
        label_fill.append(jnp.where(real, 0.0, negative_fill))
        before = jnp.where(forward, j - 1, j + 1)
        here_char = take_lanes(label_rows, jnp.clip(j, 0, LANES - 1))
        before_char = take_lanes(label_rows, jnp.clip(before, 0, LANES - 1))
        can_jump = real & (before >= 0) & (before < length) & (here_char != before_char)
        jump_fill.append(jnp.where(can_jump, 0.0, negative_fill))
        label_chars.append(jnp.where(real, here_char, -1))
        label_begin = j == jnp.where(forward, 0, label_count - 1)
        label_start.append(jnp.where(label_begin, 0.0, negative_fill))
        blank = jnp.where(forward, j, lax.rem(j + 1, span))
        blank_fill.append(jnp.where(blank < slots, 0.0, negative_fill))
        blank_begin = blank == jnp.where(forward, 0, label_count)
        blank_start.append(jnp.where(blank_begin, 0.0, negative_fill))
    blank_index = offset + slots - 1
    row_group = utterance // pack

    def frame_row(group, step):
        block = step // frames
        inside = lax.rem(step, frames)
        return jnp.broadcast_to(gathered_ref[block, group, pl.ds(inside, 1), :], shape)

    def raw_emission(step):
        raw = None
        for group in range(groups):
            early = frame_row(group, step)
            late = frame_row(group, steps - 1 - step)
            both = jnp.where(forward, early, late)
            raw = both if raw is None else jnp.where(row_group == group, both, raw)
        return raw

    def one_step(step, state):
        labels_v, blanks_v, labels_x, blanks_x = state
        raw = raw_emission(step)
        blank_emission = take_lanes(raw, blank_index)
        usable = step >= first_usable
        next_labels_v, next_blanks_v, next_labels_x, next_blanks_x = [], [], [], []
        full_labels, full_blanks = [], []
        for r in range(SPLIT):
            full_labels.append(labels_v[r] + (take_lanes(raw, label_index[r]) + label_fill[r]))
            full_blanks.append(blanks_v[r] + (blank_emission + blank_fill[r]))
            level_ref[step, r] = jnp.where(forward, full_labels[r], labels_v[r])
            level_ref[step, SPLIT + r] = jnp.where(forward, full_blanks[r], blanks_v[r])
            factor_ref[step, r] = labels_x[r]
            factor_ref[step, SPLIT + r] = blanks_x[r]
        for r in range(SPLIT):
            if r == 0:
                behind_v = pltpu.roll(full_labels[SPLIT - 1], 1, 1)
                behind_x = pltpu.roll(labels_x[SPLIT - 1], 1, 1)
            else:
                behind_v = full_labels[r - 1]
                behind_x = labels_x[r - 1]
            jump_v = behind_v + jump_fill[r]
            pivot = jnp.maximum(jnp.maximum(full_blanks[r], jump_v), full_labels[r])
            fresh_x = (
                jnp.exp(full_labels[r] - pivot) * labels_x[r]
                + jnp.exp(full_blanks[r] - pivot) * blanks_x[r]
                + jnp.exp(jump_v - pivot) * behind_x
            )
            next_labels_v.append(jnp.where(usable, pivot, label_start[r]))
            next_labels_x.append(jnp.where(usable, fresh_x, 1.0))
            pivot = jnp.maximum(full_blanks[r], behind_v)
            fresh_x = (
                jnp.exp(full_blanks[r] - pivot) * blanks_x[r]
                + jnp.exp(behind_v - pivot) * behind_x
            )
            next_blanks_v.append(jnp.where(usable, pivot, blank_start[r]))
            next_blanks_x.append(jnp.where(usable, fresh_x, 1.0))
        return (tuple(next_labels_v), tuple(next_blanks_v), tuple(next_labels_x), tuple(next_blanks_x))

    ones = (jnp.ones(shape, jnp.float32),) * SPLIT

    def run_block(block, state):
        labels_v, blanks_v = state
        full = (labels_v, blanks_v, ones, ones)
        for inner in range(UNROLL):
            full = one_step(block * UNROLL + inner, full)
        labels_v, blanks_v, labels_x, blanks_x = full
        labels_v = tuple(v + jnp.log(x) for v, x in zip(labels_v, labels_x))
        blanks_v = tuple(v + jnp.log(x) for v, x in zip(blanks_v, blanks_x))
        return labels_v, blanks_v

    lax.fori_loop(0, steps // UNROLL, run_block, (tuple(label_start), tuple(blank_start)))

    start = place_ref[0] * frames
    reverse = LANES - 1 - lane
    reverse_next = lax.rem(LANES - lane, LANES)
    chunk = 8

    def posterior_block(block, carry):
        for inner in range(chunk):
            frame = block * chunk + inner
            ahead = start + frame
            back = steps - 1 - ahead
            summed = []
            for r in range(SPLIT):
                other = SPLIT - 1 - r
                turned = take_lanes(level_ref[back, other] + jnp.log(factor_ref[back, other]), reverse)
                summed.append(
                    level_ref[ahead, r] + jnp.log(factor_ref[ahead, r])
                    + pltpu.roll(turned, utterances, 0)
                )
            for r in range(SPLIT):
                other = SPLIT + (SPLIT - r) % SPLIT
                turned = take_lanes(
                    level_ref[back, other] + jnp.log(factor_ref[back, other]),
                    reverse_next if r == 0 else reverse,
                )
                summed.append(
                    level_ref[ahead, SPLIT + r] + jnp.log(factor_ref[ahead, SPLIT + r])
                    + pltpu.roll(turned, utterances, 0)
                )
            highest = functools.reduce(jnp.maximum, summed)
            highest = jnp.max(highest, axis=1, keepdims=True)
            powers = [jnp.exp(term - highest) for term in summed]
            total = jnp.sum(sum(powers), axis=1, keepdims=True)
            scale = jnp.where(ahead < frame_count, 1.0, 0.0) / total
            for r in range(SPLIT):
                mass_ref[r, frame] = powers[r] * scale
            mass_ref[SPLIT, frame] = sum(powers[SPLIT:]) * scale
        return carry

    lax.fori_loop(0, frames // chunk, posterior_block, 0)

    vocabulary = logprob_ref.shape[1]
    chars = lax.broadcasted_iota(jnp.int32, (vocabulary, LANES), 0)
    columns = lax.broadcasted_iota(jnp.int32, (frames, vocabulary), 1)
    times = start + lax.broadcasted_iota(jnp.int32, (frames, vocabulary), 0)
    for u in range(utterances):
        mass = jnp.zeros((frames, vocabulary), jnp.float32)
        for r in range(SPLIT):
            one_hot = jnp.where(chars == label_chars[r][u:u + 1, :], 1.0, 0.0).astype(jnp.bfloat16)
            for part in three_parts(mass_ref[r, :, u, :])[:2]:
                mass += lax.dot_general(part, one_hot, BOTH_LAST, preferred_element_type=jnp.float32)
        blank_mass = jnp.sum(mass_ref[SPLIT, :, u, :], axis=1, keepdims=True)
        mass += jnp.where(columns == 0, blank_mass, 0.0)
        own = slice(u * frames, (u + 1) * frames)
        count = jnp.broadcast_to(frame_count[u:u + 1, :1], (frames, vocabulary))
        kept = jnp.where(times < count, jnp.exp(logprob_ref[own, :]) - mass, 0.0)
        logit_ref[own, :] = kept.astype(jnp.bfloat16)
    grad = logit_ref[...]
    row_ref[...] = lax.dot_general(
        grad, weight_ref[...], BOTH_LAST, preferred_element_type=jnp.float32
    ).astype(jnp.bfloat16)
    term_ref[...] = lax.dot_general(
        enc_ref[...], grad, (((0,), (0,)), ((), ())), preferred_element_type=jnp.float32
    )


def shards(enc_rows, out_weight, labels, label_count, frame_count):
    utterances, frames, width = enc_rows.shape
    vocabulary = out_weight.shape[1]
    length = labels.shape[1]
    slots = length + 1
    pack = LANES // slots
    groups = utterances // pack
    seq_count = lax.axis_size("seq")
    flat_rows = enc_rows.reshape(utterances * frames, width)
    vmem = pl.BlockSpec(memory_space=pltpu.VMEM)

    own_chars = jnp.concatenate([labels, jnp.zeros((utterances, 1), jnp.int32)], axis=1)
    segment = jnp.arange(LANES, dtype=jnp.int32)[None, :] // slots
    own_segment = jnp.arange(utterances, dtype=jnp.int32)[:, None] % pack
    chars = jnp.where(segment == own_segment, jnp.tile(own_chars, (1, pack)), -1)
    logprob, gathered = pl.pallas_call(
        functools.partial(emission_kernel, seq_count, utterances),
        out_shape=(
            jax.ShapeDtypeStruct((utterances * frames, vocabulary), jnp.float32),
            jax.ShapeDtypeStruct((seq_count, groups, frames, LANES), jnp.float32),
        ),
        in_specs=[vmem] * 3,
        out_specs=(vmem, vmem),
        scratch_shapes=[
            pltpu.SemaphoreType.DMA((seq_count - 1,)),
            pltpu.SemaphoreType.DMA((seq_count - 1,)),
        ],
        compiler_params=pltpu.CompilerParams(collective_id=0, has_side_effects=True),
        name="emission",
    )(flat_rows, out_weight, chars)

    rows = 2 * utterances
    padded = jnp.pad(labels, ((0, 0), (0, LANES - length)))
    meta = jnp.stack(
        [
            padded,
            jnp.broadcast_to(label_count[:, None], (utterances, LANES)),
            jnp.broadcast_to(frame_count[:, None], (utterances, LANES)),
        ]
    )
    meta = jnp.concatenate([meta, meta], axis=1)
    steps = seq_count * frames
    logit_grad, row_grad, term = pl.pallas_call(
        functools.partial(lattice_kernel, length, utterances),
        out_shape=(
            jax.ShapeDtypeStruct((utterances * frames, vocabulary), jnp.bfloat16),
            jax.ShapeDtypeStruct((utterances * frames, width), jnp.bfloat16),
            jax.ShapeDtypeStruct((width, vocabulary), jnp.float32),
        ),
        in_specs=[pl.BlockSpec(memory_space=pltpu.SMEM)] + [vmem] * 5,
        out_specs=(vmem, vmem, vmem),
        scratch_shapes=[
            pltpu.VMEM((steps, 2 * SPLIT, rows, LANES), jnp.float32),
            pltpu.VMEM((steps, 2 * SPLIT, rows, LANES), jnp.float32),
            pltpu.VMEM((SPLIT + 1, frames, rows, LANES), jnp.float32),
        ],
        compiler_params=pltpu.CompilerParams(vmem_limit_bytes=60 * 1024 * 1024),
        name="lattice",
    )(lax.axis_index("seq").reshape(1), gathered, meta, logprob, flat_rows, out_weight)
    batch_total = utterances * lax.axis_size("dp")
    partial_sum = lax.psum_scatter(term / batch_total, "dp", scatter_dimension=0, tiled=True)
    weight_grad = lax.psum_scatter(partial_sum, "seq", scatter_dimension=1, tiled=True)
    return (
        logit_grad.reshape(utterances, frames, vocabulary),
        row_grad.reshape(utterances, frames, width),
        weight_grad,
    )


def solution(mesh):
    placed = (P("dp", "seq", None), P(), P("dp", None), P("dp"), P("dp"))
    return jax.shard_map(
        shards,
        mesh=mesh,
        in_specs=placed,
        out_specs=(P("dp", "seq", None), P("dp", "seq", None), P("dp", "seq")),
        check_vma=False,
    )
```

```python
import functools

import jax
import jax.numpy as jnp
from jax import lax
from jax.experimental import pallas as pl
from jax.experimental.pallas import tpu as pltpu
from jax.sharding import PartitionSpec as P

negative_fill = -1e30
LANES = 128
SPLIT = 2
UNROLL = 16
MESH = pl.DeviceIdType.MESH
BOTH_LAST = (((1,), (1,)), ((), ()))


def three_parts(values):
    high = values.astype(jnp.bfloat16)
    rest = values - high.astype(jnp.float32)
    middle = rest.astype(jnp.bfloat16)
    low = (rest - middle.astype(jnp.float32)).astype(jnp.bfloat16)
    return high, middle, low


def label_table(labels_ref, table_ref):
    utterances, length = labels_ref.shape
    table_ref[...] = jnp.zeros_like(table_ref)
    table_ref[0:utterances, 0:length] = labels_ref[...]
    table_ref[utterances:2 * utterances, 0:length] = labels_ref[...]
    return table_ref[...]


def emission_kernel(seq_count, enc_ref, weight_ref, labels_ref,
                    logprob_ref, gathered_ref, table_ref, send_sems, recv_sems):
    utterances, length = labels_ref.shape
    me = lax.axis_index("seq")
    barrier = pltpu.get_barrier_semaphore()
    for step in range(1, seq_count):
        peer = lax.rem(me + step, seq_count)
        pl.semaphore_signal(barrier, inc=1, device_id={"seq": peer}, device_id_type=MESH)
    frames = enc_ref.shape[0] // utterances
    vocabulary = weight_ref.shape[1]
    groups = gathered_ref.shape[1]
    pack = utterances // groups
    logits = jnp.dot(enc_ref[...], weight_ref[...], preferred_element_type=jnp.float32)
    highest = jnp.max(logits, axis=1, keepdims=True)
    total = jnp.sum(jnp.exp(logits - highest), axis=1, keepdims=True)
    logprob = logits - (highest + jnp.log(total))
    rows = lax.broadcasted_iota(jnp.int32, (vocabulary, LANES), 0)
    table = label_table(labels_ref, table_ref)
    lane = lax.broadcasted_iota(jnp.int32, table.shape, 1)
    for group in range(groups):
        picked = jnp.zeros((frames, LANES), jnp.float32)
        for inner in range(pack):
            utterance = group * pack + inner
            begin = inner * (length + 1)
            placed = pltpu.roll(table, begin, 1) if begin else table
            inside = (lane >= begin) & (lane <= begin + length)
            placed = jnp.where(inside, placed, -1)
            one_hot = jnp.where(
                rows == placed[utterance:utterance + 1, :], 1.0, 0.0
            ).astype(jnp.bfloat16)
            mine = logprob[utterance * frames:(utterance + 1) * frames]
            for part in three_parts(mine):
                picked += jnp.dot(part, one_hot, preferred_element_type=jnp.float32)
        gathered_ref[me, group] = picked
    logprob_ref[...] = logprob
    pl.semaphore_wait(barrier, seq_count - 1)
    copies = []
    for step in range(1, seq_count):
        peer = lax.rem(me + step, seq_count)
        copy = pltpu.make_async_remote_copy(
            src_ref=gathered_ref.at[me],
            dst_ref=gathered_ref.at[me],
            send_sem=send_sems.at[step - 1],
            recv_sem=recv_sems.at[step - 1],
            device_id={"seq": peer},
            device_id_type=MESH,
        )
        copy.start()
        copies.append(copy)
    for copy in copies:
        copy.wait()


def take_lanes(values, index):
    return jnp.take_along_axis(values, index, axis=1)


def spread(count_ref, utterance):
    values = jnp.full(utterance.shape, count_ref[0], jnp.int32)
    for u in range(1, count_ref.shape[0]):
        values = jnp.where(utterance == u, count_ref[u], values)
    return values


def lattice_kernel(label_count_ref, frame_count_ref, gathered_ref, labels_ref, logprob_ref, enc_ref,
                   weight_ref, logit_ref, row_ref, term_ref, table_ref, level_ref, factor_ref,
                   mass_ref):
    utterances, length = labels_ref.shape
    seq_count, groups, frames = gathered_ref.shape[:3]
    steps = seq_count * frames
    rows = 2 * utterances
    slots = length + 1
    pack = utterances // groups
    span = LANES * SPLIT
    shape = (rows, LANES)
    row = lax.broadcasted_iota(jnp.int32, shape, 0)
    lane = lax.broadcasted_iota(jnp.int32, shape, 1)
    forward = row < utterances
    utterance = lax.rem(row, utterances)
    offset = lax.rem(utterance, pack) * slots
    label_rows = label_table(labels_ref, table_ref)
    label_count = spread(label_count_ref, utterance)
    frame_count = spread(frame_count_ref, utterance)
    first_usable = jnp.where(forward, 0, steps - frame_count)

    label_index, label_fill, jump_fill, label_start = [], [], [], []
    blank_fill, blank_start, label_chars = [], [], []
    for r in range(SPLIT):
        place = lane * SPLIT + r
        j = jnp.where(forward, place, span - 1 - place)
        real = j < length
        label_index.append(offset + jnp.clip(j, 0, slots - 1))
        label_fill.append(jnp.where(real, 0.0, negative_fill))
        before = jnp.where(forward, j - 1, j + 1)
        here_char = take_lanes(label_rows, jnp.clip(j, 0, LANES - 1))
        before_char = take_lanes(label_rows, jnp.clip(before, 0, LANES - 1))
        can_jump = real & (before >= 0) & (before < length) & (here_char != before_char)
        jump_fill.append(jnp.where(can_jump, 0.0, negative_fill))
        label_chars.append(jnp.where(real, here_char, -1))
        label_begin = j == jnp.where(forward, 0, label_count - 1)
        label_start.append(jnp.where(label_begin, 0.0, negative_fill))
        blank = jnp.where(forward, j, lax.rem(j + 1, span))
        blank_fill.append(jnp.where(blank < slots, 0.0, negative_fill))
        blank_begin = blank == jnp.where(forward, 0, label_count)
        blank_start.append(jnp.where(blank_begin, 0.0, negative_fill))
    blank_index = offset + slots - 1
    row_group = utterance // pack

    def frame_row(group, step):
        block = step // frames
        inside = lax.rem(step, frames)
        return jnp.broadcast_to(gathered_ref[block, group, pl.ds(inside, 1), :], shape)

    def raw_emission(step):
        raw = None
        for group in range(groups):
            early = frame_row(group, step)
            late = frame_row(group, steps - 1 - step)
            both = jnp.where(forward, early, late)
            raw = both if raw is None else jnp.where(row_group == group, both, raw)
        return raw

    def one_step(step, state):
        labels_v, blanks_v, labels_x, blanks_x = state
        raw = raw_emission(step)
        blank_emission = take_lanes(raw, blank_index)
        usable = step >= first_usable
        next_labels_v, next_blanks_v, next_labels_x, next_blanks_x = [], [], [], []
        full_labels, full_blanks = [], []
        for r in range(SPLIT):
            full_labels.append(labels_v[r] + (take_lanes(raw, label_index[r]) + label_fill[r]))
            full_blanks.append(blanks_v[r] + (blank_emission + blank_fill[r]))
            level_ref[step, r] = jnp.where(forward, full_labels[r], labels_v[r])
            level_ref[step, SPLIT + r] = jnp.where(forward, full_blanks[r], blanks_v[r])
            factor_ref[step, r] = labels_x[r]
            factor_ref[step, SPLIT + r] = blanks_x[r]
        for r in range(SPLIT):
            if r == 0:
                behind_v = pltpu.roll(full_labels[SPLIT - 1], 1, 1)
                behind_x = pltpu.roll(labels_x[SPLIT - 1], 1, 1)
            else:
                behind_v = full_labels[r - 1]
                behind_x = labels_x[r - 1]
            jump_v = behind_v + jump_fill[r]
            pivot = jnp.maximum(jnp.maximum(full_blanks[r], jump_v), full_labels[r])
            fresh_x = (
                jnp.exp(full_labels[r] - pivot) * labels_x[r]
                + jnp.exp(full_blanks[r] - pivot) * blanks_x[r]
                + jnp.exp(jump_v - pivot) * behind_x
            )
            next_labels_v.append(jnp.where(usable, pivot, label_start[r]))
            next_labels_x.append(jnp.where(usable, fresh_x, 1.0))
            pivot = jnp.maximum(full_blanks[r], behind_v)
            fresh_x = (
                jnp.exp(full_blanks[r] - pivot) * blanks_x[r]
                + jnp.exp(behind_v - pivot) * behind_x
            )
            next_blanks_v.append(jnp.where(usable, pivot, blank_start[r]))
            next_blanks_x.append(jnp.where(usable, fresh_x, 1.0))
        return (tuple(next_labels_v), tuple(next_blanks_v), tuple(next_labels_x), tuple(next_blanks_x))

    ones = (jnp.ones(shape, jnp.float32),) * SPLIT

    def run_block(block, state):
        labels_v, blanks_v = state
        full = (labels_v, blanks_v, ones, ones)
        for inner in range(UNROLL):
            full = one_step(block * UNROLL + inner, full)
        labels_v, blanks_v, labels_x, blanks_x = full
        labels_v = tuple(v + jnp.log(x) for v, x in zip(labels_v, labels_x))
        blanks_v = tuple(v + jnp.log(x) for v, x in zip(blanks_v, blanks_x))
        return labels_v, blanks_v

    lax.fori_loop(0, steps // UNROLL, run_block, (tuple(label_start), tuple(blank_start)))

    start = lax.axis_index("seq") * frames
    reverse = LANES - 1 - lane
    reverse_next = lax.rem(LANES - lane, LANES)
    chunk = 8

    def posterior_block(block, carry):
        for inner in range(chunk):
            frame = block * chunk + inner
            ahead = start + frame
            back = steps - 1 - ahead
            summed = []
            for r in range(SPLIT):
                other = SPLIT - 1 - r
                turned = take_lanes(level_ref[back, other] + jnp.log(factor_ref[back, other]), reverse)
                summed.append(
                    level_ref[ahead, r] + jnp.log(factor_ref[ahead, r])
                    + pltpu.roll(turned, utterances, 0)
                )
            for r in range(SPLIT):
                other = SPLIT + (SPLIT - r) % SPLIT
                turned = take_lanes(
                    level_ref[back, other] + jnp.log(factor_ref[back, other]),
                    reverse_next if r == 0 else reverse,
                )
                summed.append(
                    level_ref[ahead, SPLIT + r] + jnp.log(factor_ref[ahead, SPLIT + r])
                    + pltpu.roll(turned, utterances, 0)
                )
            highest = functools.reduce(jnp.maximum, summed)
            highest = jnp.max(highest, axis=1, keepdims=True)
            powers = [jnp.exp(term - highest) for term in summed]
            total = jnp.sum(sum(powers), axis=1, keepdims=True)
            scale = jnp.where(ahead < frame_count, 1.0, 0.0) / total
            for r in range(SPLIT):
                mass_ref[r, frame] = powers[r] * scale
            mass_ref[SPLIT, frame] = sum(powers[SPLIT:]) * scale
        return carry

    lax.fori_loop(0, frames // chunk, posterior_block, 0)

    vocabulary = logprob_ref.shape[1]
    chars = lax.broadcasted_iota(jnp.int32, (vocabulary, LANES), 0)
    columns = lax.broadcasted_iota(jnp.int32, (frames, vocabulary), 1)
    times = start + lax.broadcasted_iota(jnp.int32, (frames, vocabulary), 0)
    for u in range(utterances):
        mass = jnp.zeros((frames, vocabulary), jnp.float32)
        for r in range(SPLIT):
            one_hot = jnp.where(chars == label_chars[r][u:u + 1, :], 1.0, 0.0).astype(jnp.bfloat16)
            for part in three_parts(mass_ref[r, :, u, :])[:2]:
                mass += lax.dot_general(part, one_hot, BOTH_LAST, preferred_element_type=jnp.float32)
        blank_mass = jnp.sum(mass_ref[SPLIT, :, u, :], axis=1, keepdims=True)
        mass += jnp.where(columns == 0, blank_mass, 0.0)
        own = slice(u * frames, (u + 1) * frames)
        kept = jnp.where(times < frame_count_ref[u], jnp.exp(logprob_ref[own, :]) - mass, 0.0)
        logit_ref[own, :] = kept.astype(jnp.bfloat16)
    grad = logit_ref[...]
    row_ref[...] = lax.dot_general(
        grad, weight_ref[...], BOTH_LAST, preferred_element_type=jnp.float32
    ).astype(jnp.bfloat16)
    seq_blocks, dp_blocks, block_rows, block_columns = term_ref.shape
    for s in range(seq_blocks):
        term_ref[s] = lax.dot_general(
            enc_ref[...], grad[:, s * block_columns:(s + 1) * block_columns],
            (((0,), (0,)), ((), ())), preferred_element_type=jnp.float32,
        ).reshape(dp_blocks, block_rows, block_columns)


def binary_digits(axis, count):
    index = lax.axis_index(axis)
    digits = []
    step = 1
    while step < count:
        digit = lax.rem(index // step, 2)
        digits.append((axis, digit, index + step * (1 - 2 * digit)))
        step *= 2
    return digits


def halving_plan(seq_count, dp_count):
    seq_bits = [("seq", i) for i in range(seq_count.bit_length() - 1)]
    dp_bits = [("dp", i) for i in range(dp_count.bit_length() - 1)]
    first, others = seq_bits[:1], seq_bits[1:]
    along = first + others + dp_bits
    across = first + dp_bits[:1] + others + dp_bits[1:]
    held = seq_bits[::-1] + dp_bits[::-1]
    return held, (along, across)


def row_chunks(rows):
    quarter = -(-rows // 4 // 8) * 8
    return [(low, min(quarter, rows - low)) for low in range(0, rows, quarter)]


def reduce_kernel(seq_count, dp_count, batch_total, term_ref, out_ref, *scratch):
    digits = {
        (axis, i): entry
        for axis, count in (("seq", seq_count), ("dp", dp_count))
        for i, entry in enumerate(binary_digits(axis, count))
    }
    barrier = pltpu.get_barrier_semaphore()
    for axis, digit, partner in digits.values():
        pl.semaphore_signal(barrier, inc=1, device_id={axis: partner}, device_id_type=MESH)
    pl.semaphore_wait(barrier, len(digits))
    held, orders = halving_plan(seq_count, dp_count)
    chunks = row_chunks(term_ref.shape[-2])
    stages = len(held)
    send_sems, recv_sems = scratch[-2:]
    landing = [scratch[c * stages:(c + 1) * stages] for c in range(len(chunks))]
    current = [term_ref.at[(slice(None),) * stages + (pl.ds(low, size),)] for low, size in chunks]
    names = [list(held) for _ in chunks]
    pending = [None] * len(chunks)

    def finish(c, stage):
        copy, kept = pending[c]
        copy.wait()
        target = landing[c][stage]
        target[...] += kept[...]
        current[c] = target

    for stage in range(stages):
        for c in range(len(chunks)):
            if stage:
                finish(c, stage - 1)
            bit = orders[c % 2][stage]
            position = names[c].index(bit)
            names[c].remove(bit)
            axis, digit, partner = digits[bit]
            ahead = (slice(None),) * position
            copy = pltpu.make_async_remote_copy(
                src_ref=current[c].at[ahead + (1 - digit,)],
                dst_ref=landing[c][stage],
                send_sem=send_sems.at[c, stage],
                recv_sem=recv_sems.at[c, stage],
                device_id={axis: partner},
                device_id_type=MESH,
            )
            copy.start()
            pending[c] = (copy, current[c].at[ahead + (digit,)])
    for c, (low, size) in enumerate(chunks):
        copy, kept = pending[c]
        copy.wait()
        out_ref[low:low + size] = (landing[c][stages - 1][...] + kept[...]) / batch_total


def reduce_terms(term, batch_total):
    seq_count, dp_count, rows, columns = term.shape
    held, orders = halving_plan(seq_count, dp_count)
    stages = len(held)
    chunks = row_chunks(rows)
    scratch = []
    for low, size in chunks:
        for stage in range(stages):
            scratch.append(pltpu.VMEM((2,) * (stages - 1 - stage) + (size, columns), jnp.float32))
    vmem = pl.BlockSpec(memory_space=pltpu.VMEM)
    return pl.pallas_call(
        functools.partial(reduce_kernel, seq_count, dp_count, batch_total),
        out_shape=jax.ShapeDtypeStruct((rows, columns), jnp.float32),
        in_specs=[vmem],
        out_specs=vmem,
        scratch_shapes=scratch + [pltpu.SemaphoreType.DMA((len(chunks), stages))] * 2,
        compiler_params=pltpu.CompilerParams(
            collective_id=1, has_side_effects=True, vmem_limit_bytes=40 * 1024 * 1024
        ),
        name="reduce",
    )(term.reshape((2,) * stages + (rows, columns)))


def shards(enc_rows, out_weight, labels, label_count, frame_count):
    utterances, frames, width = enc_rows.shape
    vocabulary = out_weight.shape[1]
    length = labels.shape[1]
    slots = length + 1
    pack = LANES // slots
    groups = utterances // pack
    seq_count = lax.axis_size("seq")
    flat_rows = enc_rows.reshape(utterances * frames, width)
    vmem = pl.BlockSpec(memory_space=pltpu.VMEM)

    logprob, gathered = pl.pallas_call(
        functools.partial(emission_kernel, seq_count),
        out_shape=(
            jax.ShapeDtypeStruct((utterances * frames, vocabulary), jnp.float32),
            jax.ShapeDtypeStruct((seq_count, groups, frames, LANES), jnp.float32),
        ),
        in_specs=[vmem] * 3,
        out_specs=(vmem, vmem),
        scratch_shapes=[
            pltpu.VMEM((2 * utterances, LANES), jnp.int32),
            pltpu.SemaphoreType.DMA((seq_count - 1,)),
            pltpu.SemaphoreType.DMA((seq_count - 1,)),
        ],
        compiler_params=pltpu.CompilerParams(collective_id=0, has_side_effects=True),
        name="emission",
    )(flat_rows, out_weight, labels)

    rows = 2 * utterances
    steps = seq_count * frames
    dp_count = lax.axis_size("dp")
    smem = pl.BlockSpec(memory_space=pltpu.SMEM)
    logit_grad, row_grad, term = pl.pallas_call(
        lattice_kernel,
        out_shape=(
            jax.ShapeDtypeStruct((utterances * frames, vocabulary), jnp.bfloat16),
            jax.ShapeDtypeStruct((utterances * frames, width), jnp.bfloat16),
            jax.ShapeDtypeStruct(
                (seq_count, dp_count, width // dp_count, vocabulary // seq_count), jnp.float32
            ),
        ),
        in_specs=[smem, smem] + [vmem] * 5,
        out_specs=(vmem, vmem, vmem),
        scratch_shapes=[
            pltpu.VMEM((rows, LANES), jnp.int32),
            pltpu.VMEM((steps, 2 * SPLIT, rows, LANES), jnp.float32),
            pltpu.VMEM((steps, 2 * SPLIT, rows, LANES), jnp.float32),
            pltpu.VMEM((SPLIT + 1, frames, rows, LANES), jnp.float32),
        ],
        compiler_params=pltpu.CompilerParams(vmem_limit_bytes=60 * 1024 * 1024),
        name="lattice",
    )(label_count, frame_count, gathered, labels, logprob, flat_rows, out_weight)
    weight_grad = reduce_terms(term, utterances * dp_count)
    return (
        logit_grad.reshape(utterances, frames, vocabulary),
        row_grad.reshape(utterances, frames, width),
        weight_grad,
    )


def solution(mesh):
    placed = (P("dp", "seq", None), P(), P("dp", None), P("dp"), P("dp"))
    return jax.shard_map(
        shards,
        mesh=mesh,
        in_specs=placed,
        out_specs=(P("dp", "seq", None), P("dp", "seq", None), P("dp", "seq")),
        check_vma=False,
    )
```

```python
import functools

import jax
import jax.numpy as jnp
from jax import lax
from jax.experimental import pallas as pl
from jax.experimental.pallas import tpu as pltpu
from jax.sharding import PartitionSpec as P

negative_fill = -1e30
LANES = 128
SPLIT = 4
UNROLL = 32
MESH = pl.DeviceIdType.MESH
BOTH_LAST = (((1,), (1,)), ((), ()))


def three_parts(values):
    high = values.astype(jnp.bfloat16)
    rest = values - high.astype(jnp.float32)
    middle = rest.astype(jnp.bfloat16)
    low = (rest - middle.astype(jnp.float32)).astype(jnp.bfloat16)
    return high, middle, low


def label_table(labels_ref, table_ref):
    utterances, length = labels_ref.shape
    table_ref[...] = jnp.zeros_like(table_ref)
    table_ref[0:utterances, 0:length] = labels_ref[...]
    table_ref[utterances:2 * utterances, 0:length] = labels_ref[...]
    return table_ref[...]


def share_emissions(seq_count, enc_ref, weight_ref, labels_ref,
                    logprob_ref, gathered_ref, table_ref, send_sems, recv_sems, before_sending):
    utterances, length = labels_ref.shape
    me = lax.axis_index("seq")
    frames = enc_ref.shape[0] // utterances
    vocabulary = weight_ref.shape[1]
    groups = gathered_ref.shape[1]
    pack = utterances // groups
    logits = jnp.dot(enc_ref[...], weight_ref[...], preferred_element_type=jnp.float32)
    highest = jnp.max(logits, axis=1, keepdims=True)
    total = jnp.sum(jnp.exp(logits - highest), axis=1, keepdims=True)
    logprob = logits - (highest + jnp.log(total))
    rows = lax.broadcasted_iota(jnp.int32, (vocabulary, LANES), 0)
    table = label_table(labels_ref, table_ref)
    lane = lax.broadcasted_iota(jnp.int32, table.shape, 1)
    for group in range(groups):
        picked = jnp.zeros((frames, LANES), jnp.float32)
        for inner in range(pack):
            utterance = group * pack + inner
            begin = inner * (length + 1)
            placed = pltpu.roll(table, begin, 1) if begin else table
            inside = (lane >= begin) & (lane <= begin + length)
            placed = jnp.where(inside, placed, -1)
            one_hot = jnp.where(
                rows == placed[utterance:utterance + 1, :], 1.0, 0.0
            ).astype(jnp.bfloat16)
            mine = logprob[utterance * frames:(utterance + 1) * frames]
            for part in three_parts(mine):
                picked += jnp.dot(part, one_hot, preferred_element_type=jnp.float32)
        gathered_ref[me, group] = picked
    logprob_ref[...] = logprob
    before_sending()
    copies = []
    for step in range(1, seq_count):
        peer = lax.rem(me + step, seq_count)
        copy = pltpu.make_async_remote_copy(
            src_ref=gathered_ref.at[me],
            dst_ref=gathered_ref.at[me],
            send_sem=send_sems.at[step - 1],
            recv_sem=recv_sems.at[step - 1],
            device_id={"seq": peer},
            device_id_type=MESH,
        )
        copy.start()
        copies.append(copy)
    for copy in copies:
        copy.wait()


def take_lanes(values, index):
    return jnp.take_along_axis(values, index, axis=1)


def spread(count_ref, utterance):
    values = jnp.full(utterance.shape, count_ref[0], jnp.int32)
    for u in range(1, count_ref.shape[0]):
        values = jnp.where(utterance == u, count_ref[u], values)
    return values


def lattice_gradients(label_count_ref, frame_count_ref, gathered_ref, labels_ref, logprob_ref,
                      logit_ref, table_ref, level_ref, factor_ref, mass_ref):
    utterances, length = labels_ref.shape
    seq_count, groups, frames = gathered_ref.shape[:3]
    steps = seq_count * frames
    rows = 2 * utterances
    slots = length + 1
    pack = utterances // groups
    span = LANES * SPLIT
    shape = (rows, LANES)
    row = lax.broadcasted_iota(jnp.int32, shape, 0)
    lane = lax.broadcasted_iota(jnp.int32, shape, 1)
    forward = row < utterances
    utterance = lax.rem(row, utterances)
    offset = lax.rem(utterance, pack) * slots
    label_rows = label_table(labels_ref, table_ref)
    label_count = spread(label_count_ref, utterance)
    frame_count = spread(frame_count_ref, utterance)
    first_usable = jnp.where(forward, 0, steps - frame_count)

    label_index, label_fill, jump_fill, label_start = [], [], [], []
    blank_fill, blank_start, label_chars = [], [], []
    for r in range(SPLIT):
        place = lane * SPLIT + r
        j = jnp.where(forward, place, span - 1 - place)
        real = j < length
        label_index.append(offset + jnp.clip(j, 0, slots - 1))
        label_fill.append(jnp.where(real, 0.0, negative_fill))
        before = jnp.where(forward, j - 1, j + 1)
        here_char = take_lanes(label_rows, jnp.clip(j, 0, LANES - 1))
        before_char = take_lanes(label_rows, jnp.clip(before, 0, LANES - 1))
        can_jump = real & (before >= 0) & (before < length) & (here_char != before_char)
        jump_fill.append(jnp.where(can_jump, 0.0, negative_fill))
        label_chars.append(jnp.where(real, here_char, -1))
        label_begin = j == jnp.where(forward, 0, label_count - 1)
        label_start.append(jnp.where(label_begin, 0.0, negative_fill))
        blank = jnp.where(forward, j, lax.rem(j + 1, span))
        blank_fill.append(jnp.where(blank < slots, 0.0, negative_fill))
        blank_begin = blank == jnp.where(forward, 0, label_count)
        blank_start.append(jnp.where(blank_begin, 0.0, negative_fill))
    blank_index = offset + slots - 1
    row_group = utterance // pack

    def frame_row(group, step):
        block = step // frames
        inside = lax.rem(step, frames)
        return jnp.broadcast_to(gathered_ref[block, group, pl.ds(inside, 1), :], shape)

    def raw_emission(step):
        raw = None
        for group in range(groups):
            early = frame_row(group, step)
            late = frame_row(group, steps - 1 - step)
            both = jnp.where(forward, early, late)
            raw = both if raw is None else jnp.where(row_group == group, both, raw)
        return raw

    def one_step(step, state):
        labels_v, blanks_v, labels_x, blanks_x = state
        raw = raw_emission(step)
        blank_emission = take_lanes(raw, blank_index)
        usable = step >= first_usable
        next_labels_v, next_blanks_v, next_labels_x, next_blanks_x = [], [], [], []
        full_labels, full_blanks = [], []
        for r in range(SPLIT):
            full_labels.append(labels_v[r] + (take_lanes(raw, label_index[r]) + label_fill[r]))
            full_blanks.append(blanks_v[r] + (blank_emission + blank_fill[r]))
            level_ref[step, r] = jnp.where(forward, full_labels[r], labels_v[r])
            level_ref[step, SPLIT + r] = jnp.where(forward, full_blanks[r], blanks_v[r])
            factor_ref[step, r] = labels_x[r]
            factor_ref[step, SPLIT + r] = blanks_x[r]
        for r in range(SPLIT):
            if r == 0:
                behind_v = pltpu.roll(full_labels[SPLIT - 1], 1, 1)
                behind_x = pltpu.roll(labels_x[SPLIT - 1], 1, 1)
            else:
                behind_v = full_labels[r - 1]
                behind_x = labels_x[r - 1]
            jump_v = behind_v + jump_fill[r]
            pivot = jnp.maximum(jnp.maximum(full_blanks[r], jump_v), full_labels[r])
            fresh_x = (
                jnp.exp(full_labels[r] - pivot) * labels_x[r]
                + jnp.exp(full_blanks[r] - pivot) * blanks_x[r]
                + jnp.exp(jump_v - pivot) * behind_x
            )
            next_labels_v.append(jnp.where(usable, pivot, label_start[r]))
            next_labels_x.append(jnp.where(usable, fresh_x, 1.0))
            pivot = jnp.maximum(full_blanks[r], behind_v)
            fresh_x = (
                jnp.exp(full_blanks[r] - pivot) * blanks_x[r]
                + jnp.exp(behind_v - pivot) * behind_x
            )
            next_blanks_v.append(jnp.where(usable, pivot, blank_start[r]))
            next_blanks_x.append(jnp.where(usable, fresh_x, 1.0))
        return (tuple(next_labels_v), tuple(next_blanks_v), tuple(next_labels_x), tuple(next_blanks_x))

    ones = (jnp.ones(shape, jnp.float32),) * SPLIT

    def run_block(block, state):
        labels_v, blanks_v = state
        full = (labels_v, blanks_v, ones, ones)
        for inner in range(UNROLL):
            full = one_step(block * UNROLL + inner, full)
        labels_v, blanks_v, labels_x, blanks_x = full
        labels_v = tuple(v + jnp.log(x) for v, x in zip(labels_v, labels_x))
        blanks_v = tuple(v + jnp.log(x) for v, x in zip(blanks_v, blanks_x))
        return labels_v, blanks_v

    lax.fori_loop(0, steps // UNROLL, run_block, (tuple(label_start), tuple(blank_start)))

    start = lax.axis_index("seq") * frames
    reverse = LANES - 1 - lane
    reverse_next = lax.rem(LANES - lane, LANES)
    chunk = 8

    def posterior_block(block, carry):
        for inner in range(chunk):
            frame = block * chunk + inner
            ahead = start + frame
            back = steps - 1 - ahead
            summed = []
            for r in range(SPLIT):
                other = SPLIT - 1 - r
                turned = take_lanes(level_ref[back, other] + jnp.log(factor_ref[back, other]), reverse)
                summed.append(
                    level_ref[ahead, r] + jnp.log(factor_ref[ahead, r])
                    + pltpu.roll(turned, utterances, 0)
                )
            for r in range(SPLIT):
                other = SPLIT + (SPLIT - r) % SPLIT
                turned = take_lanes(
                    level_ref[back, other] + jnp.log(factor_ref[back, other]),
                    reverse_next if r == 0 else reverse,
                )
                summed.append(
                    level_ref[ahead, SPLIT + r] + jnp.log(factor_ref[ahead, SPLIT + r])
                    + pltpu.roll(turned, utterances, 0)
                )
            highest = functools.reduce(jnp.maximum, summed)
            highest = jnp.max(highest, axis=1, keepdims=True)
            powers = [jnp.exp(term - highest) for term in summed]
            total = jnp.sum(sum(powers), axis=1, keepdims=True)
            scale = jnp.where(ahead < frame_count, 1.0, 0.0) / total
            for r in range(SPLIT):
                mass_ref[r, frame] = powers[r] * scale
            mass_ref[SPLIT, frame] = sum(powers[SPLIT:]) * scale
        return carry

    lax.fori_loop(0, frames // chunk, posterior_block, 0)

    vocabulary = logprob_ref.shape[1]
    chars = lax.broadcasted_iota(jnp.int32, (vocabulary, LANES), 0)
    columns = lax.broadcasted_iota(jnp.int32, (frames, vocabulary), 1)
    times = start + lax.broadcasted_iota(jnp.int32, (frames, vocabulary), 0)
    for u in range(utterances):
        mass = jnp.zeros((frames, vocabulary), jnp.float32)
        for r in range(SPLIT):
            one_hot = jnp.where(chars == label_chars[r][u:u + 1, :], 1.0, 0.0).astype(jnp.bfloat16)
            for part in three_parts(mass_ref[r, :, u, :])[:2]:
                mass += lax.dot_general(part, one_hot, BOTH_LAST, preferred_element_type=jnp.float32)
        blank_mass = jnp.sum(mass_ref[SPLIT, :, u, :], axis=1, keepdims=True)
        mass += jnp.where(columns == 0, blank_mass, 0.0)
        own = slice(u * frames, (u + 1) * frames)
        kept = jnp.where(times < frame_count_ref[u], jnp.exp(logprob_ref[own, :]) - mass, 0.0)
        logit_ref[own, :] = kept.astype(jnp.bfloat16)


def binary_digits(axis, count):
    index = lax.axis_index(axis)
    digits = []
    step = 1
    while step < count:
        digit = lax.rem(index // step, 2)
        digits.append((axis, digit, index + step * (1 - 2 * digit)))
        step *= 2
    return digits


def halving_plan(seq_count, dp_count):
    seq_bits = [("seq", i) for i in range(seq_count.bit_length() - 1)]
    dp_bits = [("dp", i) for i in range(dp_count.bit_length() - 1)]
    first, others = seq_bits[:1], seq_bits[1:]
    along = first + others + dp_bits
    across = first + dp_bits[:1] + others + dp_bits[1:]
    held = others[::-1] + dp_bits[::-1]
    return held, (along, across)


def row_chunks(rows):
    quarter = -(-rows // 4 // 8) * 8
    return [(low, min(quarter, rows - low)) for low in range(0, rows, quarter)]


def fused_kernel(seq_count, dp_count, label_count_ref, frame_count_ref, enc_ref, weight_ref,
                 labels_ref, logit_ref, row_ref, out_ref, logprob_ref, gathered_ref, table_ref,
                 level_ref, factor_ref, mass_ref, sent_ref, kept_ref, share_send, share_recv,
                 send_sems, recv_sems, *landed):
    me = lax.axis_index("seq")
    digits = {
        (axis, i): entry
        for axis, count in (("seq", seq_count), ("dp", dp_count))
        for i, entry in enumerate(binary_digits(axis, count))
    }
    greeted = [("seq", lax.rem(me + step, seq_count)) for step in range(1, seq_count)]
    greeted += [(axis, partner) for axis, _, partner in digits.values() if axis == "dp"]
    barrier = pltpu.get_barrier_semaphore()
    for axis, partner in greeted:
        pl.semaphore_signal(barrier, inc=1, device_id={axis: partner}, device_id_type=MESH)

    def before_sending():
        pl.semaphore_wait(barrier, len(greeted))

    share_emissions(seq_count, enc_ref, weight_ref, labels_ref, logprob_ref, gathered_ref,
                    table_ref, share_send, share_recv, before_sending)
    lattice_gradients(label_count_ref, frame_count_ref, gathered_ref, labels_ref, logprob_ref,
                      logit_ref, table_ref, level_ref, factor_ref, mass_ref)

    grad = logit_ref[...]
    columns = sent_ref.shape[-1]
    core = digits[("seq", 0)][1]
    even = [grad[:, s * columns:(s + 1) * columns] for s in range(0, seq_count, 2)]
    odd = [grad[:, s * columns:(s + 1) * columns] for s in range(1, seq_count, 2)]

    def fill(target_ref, halves):
        product = lax.dot_general(
            enc_ref[...], jnp.concatenate(halves, axis=1), (((0,), (0,)), ((), ())),
            preferred_element_type=jnp.float32,
        )
        high = (seq_count // 2).bit_length() - 1
        for h in range(seq_count // 2):
            place = tuple((h >> (high - 1 - i)) & 1 for i in range(high))
            piece = product[:, h * columns:(h + 1) * columns]
            target_ref[place] = piece.reshape(target_ref.shape[high:])

    first = core == 0
    fill(sent_ref, [jnp.where(first, o, e) for e, o in zip(even, odd)])

    held, orders = halving_plan(seq_count, dp_count)
    rows = out_ref.shape[0]
    chunks = row_chunks(rows)
    stages = len(held) + 1
    landing = [landed[c * stages:(c + 1) * stages] for c in range(len(chunks))]
    names = [list(held) for _ in chunks]
    pending = [None] * len(chunks)

    def dense(ref, low, size):
        return ref.at[(slice(None),) * len(held) + (pl.ds(low, size),)]

    def launch(c, stage, source, kept, bit):
        axis, _, partner = digits[bit]
        copy = pltpu.make_async_remote_copy(
            src_ref=source,
            dst_ref=landing[c][stage],
            send_sem=send_sems.at[c, stage],
            recv_sem=recv_sems.at[c, stage],
            device_id={axis: partner},
            device_id_type=MESH,
        )
        copy.start()
        pending[c] = (copy, kept)

    for c, (low, size) in enumerate(chunks):
        launch(c, 0, dense(sent_ref, low, size), dense(kept_ref, low, size), ("seq", 0))
    fill(kept_ref, [jnp.where(first, e, o) for e, o in zip(even, odd)])
    row_ref[...] = lax.dot_general(
        grad, weight_ref[...], BOTH_LAST, preferred_element_type=jnp.float32
    ).astype(jnp.bfloat16)
    for stage in range(1, stages):
        for c in range(len(chunks)):
            copy, kept = pending[c]
            copy.wait()
            current = landing[c][stage - 1]
            current[...] += kept[...]
            bit = orders[c % 2][stage]
            ahead = (slice(None),) * names[c].index(bit)
            names[c].remove(bit)
            digit = digits[bit][1]
            launch(c, stage, current.at[ahead + (1 - digit,)], current.at[ahead + (digit,)], bit)
    for c, (low, size) in enumerate(chunks):
        copy, kept = pending[c]
        copy.wait()
        total = landing[c][stages - 1][...] + kept[...]
        out_ref[low:low + size] = total / (dp_count * labels_ref.shape[0])


def shards(enc_rows, out_weight, labels, label_count, frame_count):
    utterances, frames, width = enc_rows.shape
    vocabulary = out_weight.shape[1]
    length = labels.shape[1]
    slots = length + 1
    pack = LANES // slots
    groups = utterances // pack
    seq_count = lax.axis_size("seq")
    flat_rows = enc_rows.reshape(utterances * frames, width)
    vmem = pl.BlockSpec(memory_space=pltpu.VMEM)

    rows = 2 * utterances
    steps = seq_count * frames
    dp_count = lax.axis_size("dp")
    held = halving_plan(seq_count, dp_count)[0]
    block_rows, block_columns = width // dp_count, vocabulary // seq_count
    whole_block = (2,) * len(held) + (block_rows, block_columns)
    chunks = row_chunks(block_rows)
    landed = [
        pltpu.VMEM((2,) * (len(held) - stage) + (size, block_columns), jnp.float32)
        for low, size in chunks
        for stage in range(len(held) + 1)
    ]
    smem = pl.BlockSpec(memory_space=pltpu.SMEM)
    logit_grad, row_grad, weight_grad = pl.pallas_call(
        functools.partial(fused_kernel, seq_count, dp_count),
        out_shape=(
            jax.ShapeDtypeStruct((utterances * frames, vocabulary), jnp.bfloat16),
            jax.ShapeDtypeStruct((utterances * frames, width), jnp.bfloat16),
            jax.ShapeDtypeStruct((block_rows, block_columns), jnp.float32),
        ),
        in_specs=[smem, smem] + [vmem] * 3,
        out_specs=(vmem, vmem, vmem),
        scratch_shapes=[
            pltpu.VMEM((utterances * frames, vocabulary), jnp.float32),
            pltpu.VMEM((seq_count, groups, frames, LANES), jnp.float32),
            pltpu.VMEM((rows, LANES), jnp.int32),
            pltpu.VMEM((steps, 2 * SPLIT, rows, LANES), jnp.float32),
            pltpu.VMEM((steps, 2 * SPLIT, rows, LANES), jnp.float32),
            pltpu.VMEM((SPLIT + 1, frames, rows, LANES), jnp.float32),
            pltpu.VMEM(whole_block, jnp.float32),
            pltpu.VMEM(whole_block, jnp.float32),
            pltpu.SemaphoreType.DMA((seq_count - 1,)),
            pltpu.SemaphoreType.DMA((seq_count - 1,)),
            pltpu.SemaphoreType.DMA((len(chunks), len(held) + 1)),
            pltpu.SemaphoreType.DMA((len(chunks), len(held) + 1)),
        ] + landed,
        compiler_params=pltpu.CompilerParams(
            collective_id=0, has_side_effects=True, vmem_limit_bytes=60 * 1024 * 1024
        ),
        name="fused",
    )(label_count, frame_count, flat_rows, out_weight, labels)
    return (
        logit_grad.reshape(utterances, frames, vocabulary),
        row_grad.reshape(utterances, frames, width),
        weight_grad,
    )


def solution(mesh):
    placed = (P("dp", "seq", None), P(), P("dp", None), P("dp"), P("dp"))
    return jax.shard_map(
        shards,
        mesh=mesh,
        in_specs=placed,
        out_specs=(P("dp", "seq", None), P("dp", "seq", None), P("dp", "seq")),
        check_vma=False,
    )
```

```python
import functools

import jax
import jax.numpy as jnp
from jax import lax
from jax.experimental import pallas as pl
from jax.experimental.pallas import tpu as pltpu
from jax.sharding import PartitionSpec as P

negative_fill = -1e30
LANES = 128
SPLIT = 4
UNROLL = 32
MESH = pl.DeviceIdType.MESH
BOTH_LAST = (((1,), (1,)), ((), ()))


def three_parts(values):
    high = values.astype(jnp.bfloat16)
    rest = values - high.astype(jnp.float32)
    middle = rest.astype(jnp.bfloat16)
    low = (rest - middle.astype(jnp.float32)).astype(jnp.bfloat16)
    return high, middle, low


def label_table(labels_ref, table_ref):
    utterances, length = labels_ref.shape
    table_ref[...] = jnp.zeros_like(table_ref)
    table_ref[0:utterances, 0:length] = labels_ref[...]
    table_ref[utterances:2 * utterances, 0:length] = labels_ref[...]
    return table_ref[...]


def share_emissions(seq_count, enc_ref, weight_ref, labels_ref,
                    logprob_ref, gathered_ref, table_ref, send_sems, recv_sems, before_sending):
    utterances, length = labels_ref.shape
    me = lax.axis_index("seq")
    frames = enc_ref.shape[0] // utterances
    vocabulary = weight_ref.shape[1]
    groups = gathered_ref.shape[1]
    pack = utterances // groups
    logits = jnp.dot(enc_ref[...], weight_ref[...], preferred_element_type=jnp.float32)
    highest = jnp.max(logits, axis=1, keepdims=True)
    total = jnp.sum(jnp.exp(logits - highest), axis=1, keepdims=True)
    logprob = logits - (highest + jnp.log(total))
    rows = lax.broadcasted_iota(jnp.int32, (vocabulary, LANES), 0)
    table = label_table(labels_ref, table_ref)
    lane = lax.broadcasted_iota(jnp.int32, table.shape, 1)
    for group in range(groups):
        picked = jnp.zeros((frames, LANES), jnp.float32)
        for inner in range(pack):
            utterance = group * pack + inner
            begin = inner * (length + 1)
            placed = pltpu.roll(table, begin, 1) if begin else table
            inside = (lane >= begin) & (lane <= begin + length)
            placed = jnp.where(inside, placed, -1)
            one_hot = jnp.where(
                rows == placed[utterance:utterance + 1, :], 1.0, 0.0
            ).astype(jnp.bfloat16)
            mine = logprob[utterance * frames:(utterance + 1) * frames]
            for part in three_parts(mine):
                picked += jnp.dot(part, one_hot, preferred_element_type=jnp.float32)
        gathered_ref[me, group] = picked
    logprob_ref[...] = logprob
    before_sending()
    copies = []
    for step in range(1, seq_count):
        peer = lax.rem(me + step, seq_count)
        copy = pltpu.make_async_remote_copy(
            src_ref=gathered_ref.at[me],
            dst_ref=gathered_ref.at[me],
            send_sem=send_sems.at[step - 1],
            recv_sem=recv_sems.at[step - 1],
            device_id={"seq": peer},
            device_id_type=MESH,
        )
        copy.start()
        copies.append(copy)
    for copy in copies:
        copy.wait()


def take_lanes(values, index):
    return jnp.take_along_axis(values, index, axis=1)


def spread(count_ref, utterance):
    values = jnp.full(utterance.shape, count_ref[0], jnp.int32)
    for u in range(1, count_ref.shape[0]):
        values = jnp.where(utterance == u, count_ref[u], values)
    return values


def lattice_gradients(label_count_ref, frame_count_ref, gathered_ref, labels_ref, logprob_ref,
                      logit_ref, table_ref, level_ref, factor_ref, mass_ref):
    utterances, length = labels_ref.shape
    seq_count, groups, frames = gathered_ref.shape[:3]
    steps = seq_count * frames
    rows = 2 * utterances
    slots = length + 1
    pack = utterances // groups
    span = LANES * SPLIT
    shape = (rows, LANES)
    row = lax.broadcasted_iota(jnp.int32, shape, 0)
    lane = lax.broadcasted_iota(jnp.int32, shape, 1)
    forward = row < utterances
    utterance = lax.rem(row, utterances)
    offset = lax.rem(utterance, pack) * slots
    label_rows = label_table(labels_ref, table_ref)
    label_count = spread(label_count_ref, utterance)
    frame_count = spread(frame_count_ref, utterance)
    first_usable = jnp.where(forward, 0, steps - frame_count)

    label_index, label_fill, jump_fill, label_start = [], [], [], []
    blank_fill, blank_start, label_chars = [], [], []
    for r in range(SPLIT):
        place = lane * SPLIT + r
        j = jnp.where(forward, place, span - 1 - place)
        real = j < length
        label_index.append(offset + jnp.clip(j, 0, slots - 1))
        label_fill.append(jnp.where(real, 0.0, negative_fill))
        before = jnp.where(forward, j - 1, j + 1)
        here_char = take_lanes(label_rows, jnp.clip(j, 0, LANES - 1))
        before_char = take_lanes(label_rows, jnp.clip(before, 0, LANES - 1))
        can_jump = real & (before >= 0) & (before < length) & (here_char != before_char)
        jump_fill.append(jnp.where(can_jump, 0.0, negative_fill))
        label_chars.append(jnp.where(real, here_char, -1))
        label_begin = j == jnp.where(forward, 0, label_count - 1)
        label_start.append(jnp.where(label_begin, 0.0, negative_fill))
        blank = jnp.where(forward, j, lax.rem(j + 1, span))
        blank_fill.append(jnp.where(blank < slots, 0.0, negative_fill))
        blank_begin = blank == jnp.where(forward, 0, label_count)
        blank_start.append(jnp.where(blank_begin, 0.0, negative_fill))
    blank_index = offset + slots - 1
    row_group = utterance // pack

    def frame_row(group, step):
        block = step // frames
        inside = lax.rem(step, frames)
        return jnp.broadcast_to(gathered_ref[block, group, pl.ds(inside, 1), :], shape)

    def raw_emission(step):
        raw = None
        for group in range(groups):
            early = frame_row(group, step)
            late = frame_row(group, steps - 1 - step)
            both = jnp.where(forward, early, late)
            raw = both if raw is None else jnp.where(row_group == group, both, raw)
        return raw

    def one_step(step, state):
        labels_v, blanks_v, labels_x, blanks_x = state
        raw = raw_emission(step)
        blank_emission = take_lanes(raw, blank_index)
        usable = step >= first_usable
        next_labels_v, next_blanks_v, next_labels_x, next_blanks_x = [], [], [], []
        full_labels, full_blanks = [], []
        for r in range(SPLIT):
            full_labels.append(labels_v[r] + (take_lanes(raw, label_index[r]) + label_fill[r]))
            full_blanks.append(blanks_v[r] + (blank_emission + blank_fill[r]))
            level_ref[step, r] = jnp.where(forward, full_labels[r], labels_v[r])
            level_ref[step, SPLIT + r] = jnp.where(forward, full_blanks[r], blanks_v[r])
            factor_ref[step, r] = labels_x[r]
            factor_ref[step, SPLIT + r] = blanks_x[r]
        for r in range(SPLIT):
            if r == 0:
                behind_v = pltpu.roll(full_labels[SPLIT - 1], 1, 1)
                behind_x = pltpu.roll(labels_x[SPLIT - 1], 1, 1)
            else:
                behind_v = full_labels[r - 1]
                behind_x = labels_x[r - 1]
            jump_v = behind_v + jump_fill[r]
            pivot = jnp.maximum(jnp.maximum(full_blanks[r], jump_v), full_labels[r])
            fresh_x = (
                jnp.exp(full_labels[r] - pivot) * labels_x[r]
                + jnp.exp(full_blanks[r] - pivot) * blanks_x[r]
                + jnp.exp(jump_v - pivot) * behind_x
            )
            next_labels_v.append(jnp.where(usable, pivot, label_start[r]))
            next_labels_x.append(jnp.where(usable, fresh_x, 1.0))
            pivot = jnp.maximum(full_blanks[r], behind_v)
            fresh_x = (
                jnp.exp(full_blanks[r] - pivot) * blanks_x[r]
                + jnp.exp(behind_v - pivot) * behind_x
            )
            next_blanks_v.append(jnp.where(usable, pivot, blank_start[r]))
            next_blanks_x.append(jnp.where(usable, fresh_x, 1.0))
        return (tuple(next_labels_v), tuple(next_blanks_v), tuple(next_labels_x), tuple(next_blanks_x))

    ones = (jnp.ones(shape, jnp.float32),) * SPLIT

    def run_block(block, state):
        labels_v, blanks_v = state
        full = (labels_v, blanks_v, ones, ones)
        for inner in range(UNROLL):
            full = one_step(block * UNROLL + inner, full)
        labels_v, blanks_v, labels_x, blanks_x = full
        labels_v = tuple(v + jnp.log(x) for v, x in zip(labels_v, labels_x))
        blanks_v = tuple(v + jnp.log(x) for v, x in zip(blanks_v, blanks_x))
        return labels_v, blanks_v

    lax.fori_loop(0, steps // UNROLL, run_block, (tuple(label_start), tuple(blank_start)))

    start = lax.axis_index("seq") * frames
    reverse = LANES - 1 - lane
    reverse_next = lax.rem(LANES - lane, LANES)
    chunk = 8

    def posterior_block(block, carry):
        for inner in range(chunk):
            frame = block * chunk + inner
            ahead = start + frame
            back = steps - 1 - ahead
            summed = []
            for r in range(SPLIT):
                other = SPLIT - 1 - r
                turned = take_lanes(level_ref[back, other] + jnp.log(factor_ref[back, other]), reverse)
                summed.append(
                    level_ref[ahead, r] + jnp.log(factor_ref[ahead, r])
                    + pltpu.roll(turned, utterances, 0)
                )
            for r in range(SPLIT):
                other = SPLIT + (SPLIT - r) % SPLIT
                turned = take_lanes(
                    level_ref[back, other] + jnp.log(factor_ref[back, other]),
                    reverse_next if r == 0 else reverse,
                )
                summed.append(
                    level_ref[ahead, SPLIT + r] + jnp.log(factor_ref[ahead, SPLIT + r])
                    + pltpu.roll(turned, utterances, 0)
                )
            highest = functools.reduce(jnp.maximum, summed)
            highest = jnp.max(highest, axis=1, keepdims=True)
            powers = [jnp.exp(term - highest) for term in summed]
            total = jnp.sum(sum(powers), axis=1, keepdims=True)
            scale = jnp.where(ahead < frame_count, 1.0, 0.0) / total
            for r in range(SPLIT):
                mass_ref[r, frame] = powers[r] * scale
            mass_ref[SPLIT, frame] = sum(powers[SPLIT:]) * scale
        return carry

    lax.fori_loop(0, frames // chunk, posterior_block, 0)

    vocabulary = logprob_ref.shape[1]
    chars = lax.broadcasted_iota(jnp.int32, (vocabulary, LANES), 0)
    columns = lax.broadcasted_iota(jnp.int32, (frames, vocabulary), 1)
    times = start + lax.broadcasted_iota(jnp.int32, (frames, vocabulary), 0)
    for u in range(utterances):
        mass = jnp.zeros((frames, vocabulary), jnp.float32)
        for r in range(SPLIT):
            one_hot = jnp.where(chars == label_chars[r][u:u + 1, :], 1.0, 0.0).astype(jnp.bfloat16)
            for part in three_parts(mass_ref[r, :, u, :])[:2]:
                mass += lax.dot_general(part, one_hot, BOTH_LAST, preferred_element_type=jnp.float32)
        blank_mass = jnp.sum(mass_ref[SPLIT, :, u, :], axis=1, keepdims=True)
        mass += jnp.where(columns == 0, blank_mass, 0.0)
        own = slice(u * frames, (u + 1) * frames)
        kept = jnp.where(times < frame_count_ref[u], jnp.exp(logprob_ref[own, :]) - mass, 0.0)
        logit_ref[own, :] = kept.astype(jnp.bfloat16)


def binary_digits(axis, count):
    index = lax.axis_index(axis)
    digits = []
    step = 1
    while step < count:
        digit = lax.rem(index // step, 2)
        digits.append((axis, digit, index + step * (1 - 2 * digit)))
        step *= 2
    return digits


def halving_plan(seq_count, dp_count):
    seq_bits = [("seq", i) for i in range(seq_count.bit_length() - 1)]
    dp_bits = [("dp", i) for i in range(dp_count.bit_length() - 1)]
    first, others = seq_bits[:1], seq_bits[1:]
    along = first + others + dp_bits
    across = first + dp_bits[:1] + others + dp_bits[1:]
    held = others[::-1] + dp_bits[::-1]
    return held, (along, across)


def row_chunks(rows):
    quarter = -(-rows // 10 // 8) * 8
    return [(low, min(quarter, rows - low)) for low in range(0, rows, quarter)]


def fused_kernel(seq_count, dp_count, label_count_ref, frame_count_ref, enc_ref, weight_ref,
                 labels_ref, logit_ref, row_ref, out_ref, logprob_ref, gathered_ref, table_ref,
                 level_ref, factor_ref, mass_ref, sent_ref, kept_ref, share_send, share_recv,
                 send_sems, recv_sems, *landed):
    me = lax.axis_index("seq")
    digits = {
        (axis, i): entry
        for axis, count in (("seq", seq_count), ("dp", dp_count))
        for i, entry in enumerate(binary_digits(axis, count))
    }
    greeted = [("seq", lax.rem(me + step, seq_count)) for step in range(1, seq_count)]
    greeted += [(axis, partner) for axis, _, partner in digits.values() if axis == "dp"]
    barrier = pltpu.get_barrier_semaphore()
    for axis, partner in greeted:
        pl.semaphore_signal(barrier, inc=1, device_id={axis: partner}, device_id_type=MESH)

    def before_sending():
        pl.semaphore_wait(barrier, len(greeted))

    share_emissions(seq_count, enc_ref, weight_ref, labels_ref, logprob_ref, gathered_ref,
                    table_ref, share_send, share_recv, before_sending)
    lattice_gradients(label_count_ref, frame_count_ref, gathered_ref, labels_ref, logprob_ref,
                      logit_ref, table_ref, level_ref, factor_ref, mass_ref)

    grad = logit_ref[...]
    columns = sent_ref.shape[-1]
    core = digits[("seq", 0)][1]
    even = [grad[:, s * columns:(s + 1) * columns] for s in range(0, seq_count, 2)]
    odd = [grad[:, s * columns:(s + 1) * columns] for s in range(1, seq_count, 2)]

    def fill(target_ref, halves):
        product = lax.dot_general(
            enc_ref[...], jnp.concatenate(halves, axis=1), (((0,), (0,)), ((), ())),
            preferred_element_type=jnp.float32,
        )
        high = (seq_count // 2).bit_length() - 1
        for h in range(seq_count // 2):
            place = tuple((h >> (high - 1 - i)) & 1 for i in range(high))
            piece = product[:, h * columns:(h + 1) * columns]
            target_ref[place] = piece.reshape(target_ref.shape[high:])

    first = core == 0
    fill(sent_ref, [jnp.where(first, o, e) for e, o in zip(even, odd)])

    held, orders = halving_plan(seq_count, dp_count)
    rows = out_ref.shape[0]
    chunks = row_chunks(rows)
    stages = len(held) + 1
    landing = [landed[c * stages:(c + 1) * stages] for c in range(len(chunks))]
    names = [list(held) for _ in chunks]
    pending = [None] * len(chunks)

    def dense(ref, low, size):
        return ref.at[(slice(None),) * len(held) + (pl.ds(low, size),)]

    def launch(c, stage, source, kept, bit):
        axis, _, partner = digits[bit]
        copy = pltpu.make_async_remote_copy(
            src_ref=source,
            dst_ref=landing[c][stage],
            send_sem=send_sems.at[c, stage],
            recv_sem=recv_sems.at[c, stage],
            device_id={axis: partner},
            device_id_type=MESH,
        )
        copy.start()
        pending[c] = (copy, kept)

    for c, (low, size) in enumerate(chunks):
        launch(c, 0, dense(sent_ref, low, size), dense(kept_ref, low, size), ("seq", 0))
    fill(kept_ref, [jnp.where(first, e, o) for e, o in zip(even, odd)])
    row_ref[...] = lax.dot_general(
        grad, weight_ref[...], BOTH_LAST, preferred_element_type=jnp.float32
    ).astype(jnp.bfloat16)
    for stage in range(1, stages):
        for c in range(len(chunks)):
            copy, kept = pending[c]
            copy.wait()
            current = landing[c][stage - 1]
            current[...] += kept[...]
            bit = orders[c % 2][stage]
            ahead = (slice(None),) * names[c].index(bit)
            names[c].remove(bit)
            digit = digits[bit][1]
            launch(c, stage, current.at[ahead + (1 - digit,)], current.at[ahead + (digit,)], bit)
    for c, (low, size) in enumerate(chunks):
        copy, kept = pending[c]
        copy.wait()
        total = landing[c][stages - 1][...] + kept[...]
        out_ref[low:low + size] = total / (dp_count * labels_ref.shape[0])


def shards(enc_rows, out_weight, labels, label_count, frame_count):
    utterances, frames, width = enc_rows.shape
    vocabulary = out_weight.shape[1]
    length = labels.shape[1]
    slots = length + 1
    pack = LANES // slots
    groups = utterances // pack
    seq_count = lax.axis_size("seq")
    flat_rows = enc_rows.reshape(utterances * frames, width)
    vmem = pl.BlockSpec(memory_space=pltpu.VMEM)

    rows = 2 * utterances
    steps = seq_count * frames
    dp_count = lax.axis_size("dp")
    held = halving_plan(seq_count, dp_count)[0]
    block_rows, block_columns = width // dp_count, vocabulary // seq_count
    whole_block = (2,) * len(held) + (block_rows, block_columns)
    chunks = row_chunks(block_rows)
    landed = [
        pltpu.VMEM((2,) * (len(held) - stage) + (size, block_columns), jnp.float32)
        for low, size in chunks
        for stage in range(len(held) + 1)
    ]
    smem = pl.BlockSpec(memory_space=pltpu.SMEM)
    logit_grad, row_grad, weight_grad = pl.pallas_call(
        functools.partial(fused_kernel, seq_count, dp_count),
        out_shape=(
            jax.ShapeDtypeStruct((utterances * frames, vocabulary), jnp.bfloat16),
            jax.ShapeDtypeStruct((utterances * frames, width), jnp.bfloat16),
            jax.ShapeDtypeStruct((block_rows, block_columns), jnp.float32),
        ),
        in_specs=[smem, smem] + [vmem] * 3,
        out_specs=(vmem, vmem, vmem),
        scratch_shapes=[
            pltpu.VMEM((utterances * frames, vocabulary), jnp.float32),
            pltpu.VMEM((seq_count, groups, frames, LANES), jnp.float32),
            pltpu.VMEM((rows, LANES), jnp.int32),
            pltpu.VMEM((steps, 2 * SPLIT, rows, LANES), jnp.float32),
            pltpu.VMEM((steps, 2 * SPLIT, rows, LANES), jnp.float32),
            pltpu.VMEM((SPLIT + 1, frames, rows, LANES), jnp.float32),
            pltpu.VMEM(whole_block, jnp.float32),
            pltpu.VMEM(whole_block, jnp.float32),
            pltpu.SemaphoreType.DMA((seq_count - 1,)),
            pltpu.SemaphoreType.DMA((seq_count - 1,)),
            pltpu.SemaphoreType.DMA((len(chunks), len(held) + 1)),
            pltpu.SemaphoreType.DMA((len(chunks), len(held) + 1)),
        ] + landed,
        compiler_params=pltpu.CompilerParams(
            collective_id=0, has_side_effects=True, vmem_limit_bytes=60 * 1024 * 1024
        ),
        name="fused",
    )(label_count, frame_count, flat_rows, out_weight, labels)
    return (
        logit_grad.reshape(utterances, frames, vocabulary),
        row_grad.reshape(utterances, frames, width),
        weight_grad,
    )


def solution(mesh):
    placed = (P("dp", "seq", None), P(), P("dp", None), P("dp"), P("dp"))
    return jax.shard_map(
        shards,
        mesh=mesh,
        in_specs=placed,
        out_specs=(P("dp", "seq", None), P("dp", "seq", None), P("dp", "seq")),
        check_vma=False,
    )
```
